32 devices in a mesh: rep: 8 (over y, x, core), shard: 4 (over z).
Axes of the slice: x: 2, y: 2, z: 4, core: 2. Of those that a mesh axis runs over, the one named last changes fastest.
Arguments:
- tokens: bfloat16 [16384, 1024], P(('rep', 'shard')), may hold values from -6 to 6
- positions: int32 [16384], P(('rep', 'shard')), may hold values from 0 to 1535, as said below
- ln_gain: bfloat16 [1024], P('shard'), may hold values from 0.5 to 1.5
- ln_shift: bfloat16 [1024], P('shard'), may hold values from -3 to 3
- w_qkv: bfloat16 [1024, 3072], P('shard')
- w_out: bfloat16 [1024, 1024], P('shard'), may hold values from -1.5 to 1.5
- w_in: bfloat16 [1024, 4096], P('shard'), may hold values from -0.1875 to 0.1875
- b_in: bfloat16 [4096], P('shard'), may hold values from -3 to 3
- w_fc: bfloat16 [4096, 1024], P('shard'), may hold values from -0.09375 to 0.09375
- b_fc: bfloat16 [1024], P('shard'), may hold values from -3 to 3
- cotangent: bfloat16 [16384, 1024], P(('rep', 'shard')), may hold values from -6 to 6
Outputs:
- mixed: bfloat16 [16384, 1024], P(('rep', 'shard'))
- grad_tokens: bfloat16 [16384, 1024], P(('rep', 'shard'))
- grad_gain: float32 [1024], P('shard')
- grad_shift: float32 [1024], P('shard')
- grad_qkv: float32 [1024, 3072], P('shard')
- grad_out: float32 [1024, 1024], P('shard')
- grad_in: float32 [1024, 4096], P('shard')
- grad_bin: float32 [4096], P('shard')
- grad_fc: float32 [4096, 1024], P('shard')
- grad_bfc: float32 [1024], P('shard')
The draws below stay inside these ranges and needn't reach their ends.
Inputs may be any that keep to these rules, and one draw needn't show every extreme that they name: In each sequence of 2048 tokens the positions count 0, 1, 2, ... from the sequence's first token and restart at 0 exactly once, at a token in the middle half of the sequence; in the first sequence the restart is at token 512.
All inputs are finite; a program needn't handle non-finite values.
Results may differ from the reference program's by a relative error of at most 0.018.
Values may be sent and summed in bfloat16 or wider, within the bound.
No kernel may reach another device: no remote copies, remote signals or barrier semaphores. Data moves between devices by JAX's collectives and lax.ppermute only.
A program may use at most 256 MiB of HBM per device.

```python
import jax
import jax.numpy as jnp
from jax import lax

D = 1024
HEADS = 16
HD = 64
ROT = 32
FF = 4096
SEQ_LEN = 2048
SEQS = 8
TOKENS = 16384


def draw_positions(key, part):
    drawn = SEQ_LEN // 4 + jax.random.randint(key, (SEQS, 1), 0, SEQ_LEN // 2, dtype=jnp.int32)
    rows = jnp.arange(SEQS, dtype=jnp.int32)[:, None]
    cuts = jnp.where(rows == 0, SEQ_LEN // 4, drawn).astype(jnp.int32)
    index = jnp.arange(SEQ_LEN, dtype=jnp.int32)[None, :]
    placed = jnp.where(index < cuts, index, index - cuts)
    return placed.reshape(TOKENS).astype(jnp.int32)


def draw_w_qkv(key, part):
    base = jax.random.normal(key, (D, 3 * D), jnp.float32) * D ** (-0.5)
    return base.astype(jnp.bfloat16)


def level_of(key, extent, shards, least, largest):
    loudness, own = 1.0, jax.random.fold_in(key, 6)
    for position, blocks in shards:
        heights = jnp.exp(jax.random.uniform(jax.random.fold_in(own, position), (blocks,), jnp.float32, least / len(shards), largest / len(shards)))
        loudness = loudness * jnp.repeat(heights, extent[position] // blocks).reshape([-1 if axis == position else 1 for axis in range(len(extent))])
    return loudness


def bell_draw(own_key, extent, width, most, pieces=(), kind=jnp.bfloat16):
    values = jax.random.normal(own_key, extent, jnp.float32) * width
    if len(pieces) > 0:
        values = level_of(own_key, extent, pieces, -0.22, 0.18) * values
    return jnp.clip(values, min=-most, max=most).astype(kind)


def setup_inputs(seed: int = 0) -> dict:
    splits = jax.random.split(jax.random.key(seed), 12)
    tokens = bell_draw(splits[0], (TOKENS, D), 1.0, 6.0, ((0, 32),))
    positions = draw_positions(jax.random.fold_in(splits[11], 71), 0)
    ln_gain = jnp.clip(1.0 + 0.1 * jax.random.normal(splits[2], (D,), jnp.float32), 0.5, 1.5).astype(jnp.bfloat16)
    ln_shift = bell_draw(splits[3], (D,), 0.5, 3.0, ((0, 4),))
    w_qkv = draw_w_qkv(jax.random.fold_in(splits[11], 71), 0)
    w_out = bell_draw(splits[5], (D, D), (D // 64) ** -0.5, 1.5, ((0, 4),))
    w_in = bell_draw(splits[6], (D, FF), D ** -0.5, 0.1875, ((0, 4),))
    b_in = bell_draw(splits[7], (FF,), 0.5, 3.0, ((0, 4),))
    w_fc = bell_draw(splits[8], (FF, D), FF ** -0.5, 0.09375, ((0, 4),))
    b_fc = bell_draw(splits[9], (D,), 0.5, 3.0, ((0, 4),))
    cotangent = bell_draw(splits[10], (TOKENS, D), 1.0, 6.0, ((0, 32),))
    return dict(tokens=tokens, positions=positions, ln_gain=ln_gain, ln_shift=ln_shift, w_qkv=w_qkv, w_out=w_out, w_in=w_in, b_in=b_in, w_fc=w_fc, b_fc=b_fc, cotangent=cotangent)


@jax.custom_vjp
def low(v):
    return lax.optimization_barrier(v.astype(jnp.bfloat16)).astype(jnp.float32)

@jax.custom_vjp
def low_back(v):
    return v

def low_keep(v):
    return (low(v), None)

def low_pass(kept, grad):
    return (grad,)

def back_keep(v):
    return (v, None)

def back_low(kept, grad):
    return (low(grad),)
low.defvjp(low_keep, low_pass)
low_back.defvjp(back_keep, back_low)
HIGHEST = lax.Precision.HIGHEST

def rotate(field, positions):
    half = ROT // 2
    freq = 10000.0 ** (-2.0 * jnp.arange(half, dtype=jnp.float32) / ROT)
    angle = positions.astype(jnp.float32)[:, None] * freq[None, :]
    cosine = jnp.cos(angle)[:, None, :]
    sine = jnp.sin(angle)[:, None, :]
    first = field[..., :half]
    second = field[..., half:ROT]
    return jnp.concatenate([first * cosine - second * sine, second * cosine + first * sine, field[..., ROT:]], axis=-1)

def gelu_tanh(value):
    return 0.5 * value * (1.0 + jnp.tanh(0.7978845608028654 * (value + 0.044715 * value * value * value)))

def attend_sequence(item):
    queries, keys, values, positions = item
    length = queries.shape[0]
    index = jnp.arange(length, dtype=jnp.int32)
    first = index - positions
    allowed = (index[None, :] <= index[:, None]) & (index[None, :] >= first[:, None])
    scores = jnp.einsum('qhd,khd->hqk', queries, keys, precision=HIGHEST) * HD ** (-0.5)
    scores = low_back(jnp.where(allowed[None], scores, -1e+30))
    probs = jax.nn.softmax(scores, axis=-1)
    return jnp.einsum('hqk,khd->qhd', low(probs), values, precision=HIGHEST)

def forward(tokens, ln_gain, ln_shift, w_qkv, w_out, w_in, b_in, w_fc, b_fc, positions):
    count = tokens.shape[0]
    mean = lax.optimization_barrier(jnp.mean(tokens, axis=-1, keepdims=True))
    centered = tokens - mean
    variance = lax.optimization_barrier(jnp.mean(centered * centered, axis=-1, keepdims=True))
    normed = low(centered * lax.rsqrt(variance + 1e-05) * ln_gain + ln_shift)
    mixed_qkv = low_back(jnp.dot(normed, w_qkv, precision=HIGHEST))
    queries = low(rotate(mixed_qkv[:, :D].reshape(count, HEADS, HD), positions))
    keys = low(rotate(mixed_qkv[:, D:2 * D].reshape(count, HEADS, HD), positions))
    values = low(mixed_qkv[:, 2 * D:].reshape(count, HEADS, HD))
    shape4 = (SEQS, SEQ_LEN, HEADS, HD)
    attended = lax.map(jax.checkpoint(attend_sequence), (queries.reshape(shape4), keys.reshape(shape4), values.reshape(shape4), positions.reshape(SEQS, SEQ_LEN)))
    attended = low(low_back(attended.reshape(count, D)))
    attn_out = jnp.dot(attended, w_out, precision=HIGHEST)
    hidden_pre = low_back(jnp.dot(normed, w_in, precision=HIGHEST) + b_in)
    activated = low(gelu_tanh(hidden_pre))
    mlp_out = jnp.dot(activated, w_fc, precision=HIGHEST) + b_fc
    return tokens + attn_out + mlp_out

def reference(tokens, positions, ln_gain, ln_shift, w_qkv, w_out, w_in, b_in, w_fc, b_fc, cotangent):
    floats = [a.astype(jnp.float32) for a in (tokens, ln_gain, ln_shift, w_qkv, w_out, w_in, b_in, w_fc, b_fc)]
    result, pull = jax.vjp(lambda *values: forward(*values, positions), *floats)
    grads = pull(cotangent.astype(jnp.float32))
    return (result.astype(jnp.bfloat16), grads[0].astype(jnp.bfloat16), grads[1], grads[2], grads[3], grads[4], grads[5], grads[6], grads[7], grads[8])
```

```python
import functools

import jax
import jax.numpy as jnp
from jax import lax
from jax.experimental import pallas as pl
from jax.experimental.pallas import tpu as pltpu
from jax.sharding import PartitionSpec as P

D = 1024
HEADS = 16
HD = 64
ROT = 32
FF = 4096
EPS = 1e-05

SHARDS = 4
PAIRS = 4
HALF = D // 2
CHUNKS = 2
WIDE = FF // 2 // CHUNKS
PART = WIDE // SHARDS
masked_score = -1e30
low = jnp.bfloat16
full = jnp.float32
contract_rows = (((0,), (0,)), ((), ()))
contract_cols = (((1,), (1,)), ((), ()))
VMEM_LIMIT = 60 * 1024 * 1024


def dot(a, b):
    return jnp.dot(a, b, preferred_element_type=full)


def dot_t(a, b):
    return lax.dot_general(a, b, contract_cols, preferred_element_type=full)


def t_dot(a, b):
    return lax.dot_general(a, b, contract_rows, preferred_element_type=full)


def start_fetch(sc, own, pieces, target, row_of, sems):
    z, j = sc[0], sc[1]
    copies = []
    for ref, row in own:
        copies.append((ref, row, ref.shape[0]))
    for s in range(1, SHARDS):
        for p in range(4):
            ref = pieces[(s - 1) * 4 + p]
            copies.append((ref, row_of((z + s) % SHARDS, j ^ p), ref.shape[0]))
    started = []
    for i, (ref, row, count) in enumerate(copies):
        move = pltpu.make_async_copy(
            ref, target.at[pl.ds(pl.multiple_of(row, 32), count), :], sems.at[i]
        )
        move.start()
        started.append(move)
    return started


def mlp_row(zz, jj):
    return (jj // 2) * D + zz * 256 + (jj % 2) * 128


def mlp_kernel(sc, normed, dy, bias, own, *rest):
    pieces = rest[:12]
    mlp_o, dn_o, g_o, gb_o, w, act, dup, sems = rest[12:]
    step = pl.program_id(0)
    tile = mlp_o.shape[0]
    tiles = normed.shape[0] // tile

    @pl.when(step == 0)
    def _():
        z = sc[0]
        moves = start_fetch(
            sc,
            [(own.at[pl.ds(0, 256), :], z * 256), (own.at[pl.ds(256, 256), :], D + z * 256)],
            pieces,
            w,
            mlp_row,
            sems,
        )
        for move in moves:
            move.wait()
        gb_o[...] = jnp.zeros_like(gb_o)

    @pl.when(step < tiles)
    def _():
        rows = pl.ds(pl.multiple_of(step * tile, tile), tile)
        up = dot(normed[rows, :], w[:D, :]) + bias[...]
        d_act = dot_t(dy[rows, :], w[D:, :])
        square = up * up
        inner = 0.7978845608028654 * (up + 0.044715 * square * up)
        th = jnp.tanh(inner)
        one = 0.5 * (1.0 + th)
        slope = one + (0.5 * up) * (1.0 - th * th) * (
            0.7978845608028654 + (0.7978845608028654 * 3.0 * 0.044715) * square
        )
        a16 = (up * one).astype(low)
        du = (d_act * slope).astype(low)
        act[rows, :] = a16
        dup[rows, :] = du
        gb_o[...] += jnp.sum(du.astype(full), axis=0, keepdims=True)
        mlp_o[...] = dot(a16, w[D:, :]).astype(low)
        dn_o[...] = dot_t(du, w[:D, :]).astype(low)

    @pl.when((step >= tiles) & (step < tiles + 4))
    def _():
        cols = pl.ds(pl.multiple_of((step - tiles) * 256, 256), 256)
        g_o[...] = t_dot(normed[:, cols], dup[...]).astype(low)

    @pl.when(step >= tiles + 4)
    def _():
        cols = pl.ds(pl.multiple_of((step - tiles - 4) * 256, 256), 256)
        g_o[...] = t_dot(act[:, cols], dy[...]).astype(low)


def whole(shape):
    return pl.BlockSpec(
        shape, lambda *_: (0,) * len(shape), pipeline_mode=pl.Buffered(1)
    )


ANY = pl.BlockSpec(memory_space=pl.ANY)


def mlp_call(sc, normed, dy, bias, own, pieces):
    rows = normed.shape[0]
    tile = 256
    tiles = rows // tile
    return pl.pallas_call(
        mlp_kernel,
        out_shape=(
            jax.ShapeDtypeStruct((rows, D), low),
            jax.ShapeDtypeStruct((rows, D), low),
            jax.ShapeDtypeStruct((2 * D, WIDE), low),
            jax.ShapeDtypeStruct((1, WIDE), full),
        ),
        grid_spec=pltpu.PrefetchScalarGridSpec(
            num_scalar_prefetch=1,
            grid=(tiles + 8,),
            in_specs=[whole((rows, D)), whole((rows, D)), whole((1, WIDE)), ANY] + [ANY] * 12,
            out_specs=[
                pl.BlockSpec((tile, D), lambda i, sc: (jnp.minimum(i, tiles - 1), 0)),
                pl.BlockSpec((tile, D), lambda i, sc: (jnp.minimum(i, tiles - 1), 0)),
                pl.BlockSpec((256, WIDE), lambda i, sc: (jnp.maximum(i - tiles, 0), 0)),
                pl.BlockSpec((1, WIDE), lambda i, sc: (0, 0)),
            ],
            scratch_shapes=[
                pltpu.VMEM((2 * D, WIDE), low),
                pltpu.VMEM((rows, WIDE), low),
                pltpu.VMEM((rows, WIDE), low),
                pltpu.SemaphoreType.DMA((14,)),
            ],
        ),
        compiler_params=pltpu.CompilerParams(
            dimension_semantics=("arbitrary",), vmem_limit_bytes=VMEM_LIMIT
        ),
        cost_estimate=pl.CostEstimate(
            flops=12 * rows * D * WIDE, bytes_accessed=24 << 20, transcendentals=rows * WIDE
        ),
        name="mlp",
    )(sc, normed, dy, bias, own, *pieces)


def swap_halves(t):
    lane = lax.broadcasted_iota(jnp.int32, t.shape, 1) % HD
    return jnp.where(lane < ROT // 2, pltpu.roll(t, 128 - ROT // 2, 1), pltpu.roll(t, ROT // 2, 1))


def qkv_row(zz, jj):
    return zz * 256 + jj * 64


def out_row(zz, jj):
    return zz * 128 + jj * 32


def proj_kernel(mine, sc, normed, dy, cos, sin, own_qkv, own_out, *rest):
    pq, po = rest[:12], rest[12:24]
    if mine:
        k_o, v_o, q_o, da_o, wq, wo, sems = rest[24:]
    else:
        k_o, v_o, wq, sems = rest[24:]
    step = pl.program_id(0)

    @pl.when(step == 0)
    def _():
        z = sc[0]
        moves = start_fetch(sc, [(own_qkv, z * 256)], pq, wq, qkv_row, sems.at[0])
        if mine:
            moves += start_fetch(sc, [(own_out, z * 128)], po, wo, out_row, sems.at[1])
        for move in moves:
            move.wait()

    first = 0 if mine else HALF
    mixed = dot(normed[...], wq[:, first:])
    c, s = cos[...], sin[...]

    def turned(base):
        outs = []
        for pair in range(PAIRS):
            t = mixed[:, base + pair * 128 : base + (pair + 1) * 128]
            outs.append((t * c + swap_halves(t) * s).astype(low))
        return jnp.concatenate(outs, axis=1)

    if mine:
        q_o[...] = turned(0)
        da_o[...] = dot_t(dy[...], wo[...]).astype(low)
    k_o[...] = turned(HALF - first)
    v_o[...] = mixed[:, 2 * HALF - first :].astype(low)


def proj_call(mine, sc, normed, dy, cos, sin, own_qkv, own_out, pq, po):
    rows = normed.shape[0]
    tile = 256
    grid = rows // tile
    outs = [jax.ShapeDtypeStruct((rows, HALF), low)] * (4 if mine else 2)
    spec = pl.BlockSpec((tile, HALF), lambda i, sc: (i, 0))
    wide = pl.BlockSpec((tile, D), lambda i, sc: (i, 0))
    table = pl.BlockSpec((tile, 128), lambda i, sc: (i, 0))
    scratch = [pltpu.VMEM((D, 3 * HALF), low)]
    if mine:
        scratch.append(pltpu.VMEM((HALF, D), low))
    return pl.pallas_call(
        functools.partial(proj_kernel, mine),
        out_shape=outs,
        grid_spec=pltpu.PrefetchScalarGridSpec(
            num_scalar_prefetch=1,
            grid=(grid,),
            in_specs=[wide, wide if mine else ANY, table, table, ANY, ANY] + [ANY] * 24,
            out_specs=[spec] * len(outs),
            scratch_shapes=scratch + [pltpu.SemaphoreType.DMA((2, 13))],
        ),
        compiler_params=pltpu.CompilerParams(
            dimension_semantics=("arbitrary",), vmem_limit_bytes=VMEM_LIMIT
        ),
        cost_estimate=pl.CostEstimate(
            flops=2 * rows * D * HALF * (4 if mine else 2),
            bytes_accessed=12 << 20,
            transcendentals=0,
        ),
        name="proj_mine" if mine else "proj_prior",
    )(sc, normed, dy, cos, sin, own_qkv, own_out, *pq, *po)


def attend_kernel(sc, q, da, ko, kp, vo, vp, first, cos_o, sin_o, cos_p, sin_p, *rest):
    att_o, dq_o, dko_o, dkp_o, dvo_o, dvp_o, bias, dkt, dvt = rest
    rows = q.shape[1]
    keys = rows * 3
    z = sc[0]

    @pl.when(pl.program_id(1) == 0)
    def _():
        start = (z - 2) * rows
        tile = 64

        def fill(i, unused):
            at = pl.ds(pl.multiple_of(i * tile, tile), tile)
            key = start + lax.broadcasted_iota(jnp.int32, (tile, keys), 1)
            query = z * rows + i * tile + lax.broadcasted_iota(jnp.int32, (tile, keys), 0)
            allowed = (key <= query) & (key >= first[0, at, :])
            bias[at, :] = jnp.where(allowed, 0.0, masked_score)
            return unused

        lax.fori_loop(0, rows // tile, fill, 0)

    k = jnp.concatenate([kp[0], ko[0]], axis=0)
    v = jnp.concatenate([vp[0], vo[0]], axis=0)
    scale = HD ** (-0.5)
    tile = rows // 2
    for t in range(2):
        at = slice(t * tile, (t + 1) * tile)
        count = keys - (tile if t == 0 else 0)
        q_t = q[0, at, :]
        da_t = da[0, at, :]
        lane = lax.broadcasted_iota(jnp.int32, (tile, 128), 1)
        k_t, v_t = k[:count], v[:count]
        outs, dqs = [], []
        dk_sum, dv_sum = None, None
        for h in range(2):
            inside = (lane // HD) == h
            qh = jnp.where(inside, q_t.astype(full) * scale, 0.0).astype(low)
            dh = jnp.where(inside, da_t.astype(full), 0.0)
            dh16 = dh.astype(low)
            s = dot_t(qh, k_t) + bias[at, :count]
            peak = jnp.max(s, axis=-1, keepdims=True)
            e = jnp.exp(s - peak)
            p = e * (1.0 / jnp.sum(e, axis=-1, keepdims=True))
            p16 = p.astype(low)
            o = dot(p16, v_t)
            delta = jnp.sum(dh * o, axis=-1, keepdims=True)
            ds = (p * (dot_t(dh16, v_t) - delta)).astype(low)
            dqs.append(dot(ds, k_t))
            outs.append(o)
            dk_h = t_dot(qh, ds)
            dv_h = t_dot(dh16, p16)
            dk_sum = dk_h if dk_sum is None else dk_sum + dk_h
            dv_sum = dv_h if dv_sum is None else dv_sum + dv_h
        left = lane < HD
        att_o[0, at, :] = jnp.where(left, outs[0], outs[1]).astype(low)
        dq = jnp.where(left, dqs[0], dqs[1]) * scale
        c, sn = cos_o[0, at, :], sin_o[0, at, :]
        dq_o[0, at, :] = (dq * c - swap_halves(dq) * sn).astype(low)
        if t == 0:
            dkt[:, :count] = dk_sum
            dvt[:, :count] = dv_sum
            dkt[:, count:] = jnp.zeros((128, keys - count), full)
            dvt[:, count:] = jnp.zeros((128, keys - count), full)
        else:
            dkt[...] += dk_sum
            dvt[...] += dv_sum
    dk = dkt[...].T
    dv = dvt[...].T
    prior = 2 * rows
    dk_p, dk_m = dk[:prior], dk[prior:]
    dkp_o[0] = (dk_p * cos_p[0] - swap_halves(dk_p) * sin_p[0]).astype(low)
    dko_o[0] = (dk_m * cos_o[0] - swap_halves(dk_m) * sin_o[0]).astype(low)
    dvp_o[0] = dv[:prior].astype(low)
    dvo_o[0] = dv[prior:].astype(low)


def attend_call(sc, q, da, ko, kp, vo, vp, first, cos_o, sin_o, cos_p, sin_p):
    seqs, rows = q.shape[0], q.shape[1]
    one = pl.BlockSpec((1, rows, 128), lambda i, p, sc: (i, 0, p))
    two = pl.BlockSpec((1, 2 * rows, 128), lambda i, p, sc: (i, 0, p))
    col = pl.BlockSpec((1, rows, 1), lambda i, p, sc: (i, 0, 0))
    tab1 = pl.BlockSpec((1, rows, 128), lambda i, p, sc: (i, 0, 0))
    tab2 = pl.BlockSpec((1, 2 * rows, 128), lambda i, p, sc: (i, 0, 0))
    mine = jax.ShapeDtypeStruct((seqs, rows, HALF), low)
    prior = jax.ShapeDtypeStruct((seqs, 2 * rows, HALF), low)
    return pl.pallas_call(
        attend_kernel,
        out_shape=(mine, mine, mine, prior, mine, prior),
        grid_spec=pltpu.PrefetchScalarGridSpec(
            num_scalar_prefetch=1,
            grid=(seqs, PAIRS),
            in_specs=[one, one, one, two, one, two, col, tab1, tab1, tab2, tab2],
            out_specs=[one, one, one, two, one, two],
            scratch_shapes=[
                pltpu.VMEM((rows, 3 * rows), full),
                pltpu.VMEM((128, 3 * rows), full),
                pltpu.VMEM((128, 3 * rows), full),
            ],
        ),
        compiler_params=pltpu.CompilerParams(
            dimension_semantics=("arbitrary", "arbitrary"), vmem_limit_bytes=VMEM_LIMIT
        ),
        cost_estimate=pl.CostEstimate(
            flops=12 * seqs * rows * 3 * rows * 256 * 8,
            bytes_accessed=20 << 20,
            transcendentals=seqs * rows * rows * 3 * 8,
        ),
        name="attend",
    )(sc, q, da, ko, kp, vo, vp, first, cos_o, sin_o, cos_p, sin_p)


def back_kernel(
    sc, normed, before, dy, att, dq, dko, dvo, dkp, dvp, own_qkv, own_out, *rest
):
    pq, po = rest[:12], rest[12:24]
    out_o, dn_o, dnp_o, gq_o, go_o, wq, wo, sems = rest[24:]
    step = pl.program_id(0)
    tile = out_o.shape[0]
    mine = normed.shape[0] // tile
    prior = before.shape[0] // tile

    @pl.when(step == 0)
    def _():
        z = sc[0]
        moves = start_fetch(sc, [(own_qkv, z * 256)], pq, wq, qkv_row, sems.at[0])
        moves += start_fetch(sc, [(own_out, z * 128)], po, wo, out_row, sems.at[1])
        for move in moves:
            move.wait()

    @pl.when(step < prior)
    def _():
        at = pl.ds(pl.multiple_of(step * tile, tile), tile)
        dnp_o[...] = (
            dot_t(dkp[at, :], wq[:, HALF : 2 * HALF]) + dot_t(dvp[at, :], wq[:, 2 * HALF :])
        ).astype(low)

    @pl.when((step >= prior) & (step < prior + mine))
    def _():
        at = pl.ds(pl.multiple_of((step - prior) * tile, tile), tile)
        dn_o[...] = (
            dot_t(dq[at, :], wq[:, :HALF])
            + dot_t(dko[at, :], wq[:, HALF : 2 * HALF])
            + dot_t(dvo[at, :], wq[:, 2 * HALF :])
        ).astype(low)
        out_o[...] = dot(att[at, :], wo[...]).astype(low)

    base = prior + mine

    @pl.when((step >= base) & (step < base + 4))
    def _():
        cols = pl.ds(pl.multiple_of((step - base) * 256, 256), 256)
        n_m, n_p = normed[:, cols], before[:, cols]
        gq_o[:, :HALF] = t_dot(n_m, dq[...]).astype(low)
        gq_o[:, HALF : 2 * HALF] = (t_dot(n_m, dko[...]) + t_dot(n_p, dkp[...])).astype(low)
        gq_o[:, 2 * HALF :] = (t_dot(n_m, dvo[...]) + t_dot(n_p, dvp[...])).astype(low)

    @pl.when(step >= base + 4)
    def _():
        cols = pl.ds(pl.multiple_of((step - base - 4) * 256, 256), 256)
        go_o[...] = t_dot(att[:, cols], dy[...]).astype(low)


def back_call(sc, normed, before, dy, att, dq, dko, dvo, dkp, dvp, own_qkv, own_out, pq, po):
    rows, early = normed.shape[0], before.shape[0]
    tile = 256
    mine, prior = rows // tile, early // tile
    base = mine + prior
    wide = lambda f: pl.BlockSpec((tile, D), lambda i, sc: (f(i), 0))
    clip = jnp.clip
    return pl.pallas_call(
        back_kernel,
        out_shape=(
            jax.ShapeDtypeStruct((rows, D), low),
            jax.ShapeDtypeStruct((rows, D), low),
            jax.ShapeDtypeStruct((early, D), low),
            jax.ShapeDtypeStruct((D, 3 * HALF), low),
            jax.ShapeDtypeStruct((HALF, D), low),
        ),
        grid_spec=pltpu.PrefetchScalarGridSpec(
            num_scalar_prefetch=1,
            grid=(base + 6,),
            in_specs=[
                whole((rows, D)),
                whole((early, D)),
                whole((rows, D)),
                whole((rows, HALF)),
                whole((rows, HALF)),
                whole((rows, HALF)),
                whole((rows, HALF)),
                whole((early, HALF)),
                whole((early, HALF)),
            ]
            + [ANY] * 26,
            out_specs=[
                wide(lambda i: clip(i - prior, 0, mine - 1)),
                wide(lambda i: clip(i - prior, 0, mine - 1)),
                wide(lambda i: clip(i, 0, prior - 1)),
                pl.BlockSpec((256, 3 * HALF), lambda i, sc: (clip(i - base, 0, 3), 0)),
                pl.BlockSpec((256, D), lambda i, sc: (clip(i - base - 4, 0, 1), 0)),
            ],
            scratch_shapes=[
                pltpu.VMEM((D, 3 * HALF), low),
                pltpu.VMEM((HALF, D), low),
                pltpu.SemaphoreType.DMA((2, 13)),
            ],
        ),
        compiler_params=pltpu.CompilerParams(
            dimension_semantics=("arbitrary",), vmem_limit_bytes=VMEM_LIMIT
        ),
        cost_estimate=pl.CostEstimate(
            flops=2 * D * HALF * (8 * rows + 4 * early),
            bytes_accessed=40 << 20,
            transcendentals=0,
        ),
        name="back",
    )(sc, normed, before, dy, att, dq, dko, dvo, dkp, dvp, own_qkv, own_out, *pq, *po)


def on_device(
    reps, tokens, positions, ln_gain, ln_shift, w_qkv, w_out, w_in, b_in, w_fc, b_fc, cotangent
):
    rows = tokens.shape[0]
    z = lax.axis_index("shard")
    r = lax.axis_index("rep")
    c = r % 2
    x = (r // 2) % 2
    y = (r // 4) % 2
    j = (r // 2) % 4
    sc = jnp.stack([z, j]).astype(jnp.int32)

    def swap(a, bit):
        return lax.ppermute(a, "rep", [(i, i ^ bit) for i in range(reps)])

    def from_shard(a, s):
        return lax.ppermute(a, "shard", [(i, (i - s) % SHARDS) for i in range(SHARDS)])

    def to_shard(a, s):
        return lax.ppermute(a, "shard", [(i, (i + s) % SHARDS) for i in range(SHARDS)])

    def upward(a):
        return lax.ppermute(a, "shard", [(i, i + 1) for i in range(SHARDS - 1)])

    def downward(a):
        return lax.ppermute(a, "shard", [(i + 1, i) for i in range(SHARDS - 1)])

    def spread(a, x_first):
        if x_first:
            by_x = swap(a, 2)
            return (a, by_x, swap(a, 4), swap(by_x, 4))
        by_y = swap(a, 4)
        return (a, swap(a, 2), by_y, swap(by_y, 2))

    def gather(a, x_first):
        quarter = a.shape[0] // 4
        mine = lax.dynamic_slice_in_dim(a, j * quarter, quarter, 0)
        pieces = []
        for s in range(1, SHARDS):
            pieces.extend(spread(from_shard(mine, s), x_first ^ (s == 2)))
        return pieces

    def pick(a, at, axis):
        return lax.dynamic_index_in_dim(a, at, axis, keepdims=False)

    def add(a, b):
        return (a.astype(full) + b.astype(full)).astype(low)

    vec = jnp.concatenate([ln_gain, ln_shift, b_fc, b_in]).reshape(1, -1)
    vecs = [vec] + [from_shard(vec, s) for s in range(1, SHARDS)]
    stacked = jnp.concatenate(vecs + vecs[:-1], axis=0)
    vecs = lax.dynamic_slice_in_dim(stacked, (SHARDS - z) % SHARDS, SHARDS, 0)
    quart = D // SHARDS
    gain = vecs[:, :quart].reshape(D).astype(full)
    shift = vecs[:, quart : 2 * quart].reshape(D).astype(full)
    bfc = vecs[:, 2 * quart : 3 * quart].reshape(D).astype(full)
    bin_half = pick(vecs[:, 3 * quart :].astype(full).reshape(SHARDS, 2, CHUNKS, PART), c, 1)

    in_half = pick(w_in.reshape(quart, SHARDS, 2, CHUNKS, PART), c, 2)
    fc_half = pick(w_fc.reshape(2, CHUNKS, PART, D), c, 0)
    qkv_half = pick(w_qkv.reshape(quart, 3 * PAIRS, 2, 128), c, 2).reshape(quart, 3 * HALF)
    out_half = pick(w_out.reshape(2, 128, D), c, 0)
    packs = [
        jnp.concatenate([in_half[:, :, k].reshape(quart, WIDE), fc_half[k]], axis=0)
        for k in range(CHUNKS)
    ]

    other = swap(tokens, 1)
    dy_other = swap(cotangent, 1)
    pos_other = swap(positions, 1)
    got = [gather(packs[0], True)]
    one_up = upward(tokens)
    got.append(gather(packs[1], False))
    two_up = upward(one_up)
    got_qkv = gather(qkv_half, True)
    got_out = gather(out_half, False)

    def normalize(values):
        v = values.astype(full)
        mean = jnp.mean(v, axis=-1, keepdims=True)
        centered = v - mean
        rstd = lax.rsqrt(jnp.mean(centered * centered, axis=-1, keepdims=True) + EPS)
        return mean, rstd, (centered * rstd * gain + shift).astype(low)

    both = jnp.stack([tokens, other])
    dy = jnp.concatenate([cotangent, dy_other], axis=0)
    mean, rstd, normed = normalize(both)
    normed = normed.reshape(2 * rows, D)
    early = jnp.stack([two_up, one_up])
    early = jnp.stack([early, swap(early, 1)])
    mean_p, rstd_p, before = normalize(early)
    before = before.reshape(4 * rows, D)

    half = ROT // 2
    freq = 10000.0 ** (-2.0 * jnp.arange(half, dtype=full) / ROT)
    lane = jnp.arange(128) % HD
    freq_lane = jnp.where(lane < ROT, freq[lane % half], 0.0)
    sign = jnp.where(lane < half, -1.0, jnp.where(lane < ROT, 1.0, 0.0)).astype(full)
    pos = jnp.stack([positions, pos_other])
    index = z * rows + jnp.arange(rows, dtype=jnp.int32)
    first = index[None, :] - pos
    key_index = (z - 2) * rows + jnp.arange(2 * rows, dtype=jnp.int32)
    pos_p = jnp.maximum(key_index[None, :] - first[:, :1], 0)

    def tables(p):
        angle = p.astype(full)[..., None] * freq_lane
        return jnp.cos(angle), jnp.sin(angle) * sign

    cos_o, sin_o = tables(pos)
    cos_p, sin_p = tables(pos_p)

    def reduce(parts, x_first):
        for bit, axis in ((2, 2), (4, 0)) if x_first else ((4, 0), (2, 1)):
            at = x if bit == 2 else y
            kept, sent = pick(parts, at, axis), pick(parts, 1 - at, axis)
            parts = add(kept, swap(sent, bit))
        total = pick(parts, z, 0).astype(full)
        for s in range(1, SHARDS):
            total = total + to_shard(pick(parts, (z + s) % SHARDS, 0), s).astype(full)
        total = total.astype(low)
        bit = 8
        while bit < reps:
            total = add(total, swap(total, bit))
            bit *= 2
        return total

    def ordered(pieces):
        a, b, e, d = pieces
        swap_x = x == 1
        a, b = jnp.where(swap_x, b, a), jnp.where(swap_x, a, b)
        e, d = jnp.where(swap_x, d, e), jnp.where(swap_x, e, d)
        swap_y = y == 1
        return jnp.stack(
            [
                jnp.where(swap_y, e, a),
                jnp.where(swap_y, d, b),
                jnp.where(swap_y, a, e),
                jnp.where(swap_y, b, d),
            ]
        )

    def finish(total, x_first):
        mine = ordered(spread(total, x_first))
        theirs = swap(mine, 1)
        return jnp.where(c == 0, jnp.stack([mine, theirs]), jnp.stack([theirs, mine]))

    mlp_sum, dn_sum, grads_mlp, bin_parts = [], [], [], []
    for k in range(CHUNKS):
        bias = bin_half[:, k].reshape(1, WIDE)
        mlp_o, dn_o, g, gb = mlp_call(sc, normed, dy, bias, packs[k], got[k])
        mlp_sum.append(mlp_o)
        dn_sum.append(dn_o)
        bin_parts.append(gb.reshape(SHARDS, PART))
        parts = g.reshape(2, SHARDS, 2, 128, WIDE)
        grads_mlp.append(finish(reduce(parts, k == 0), k == 0))

    flat = lambda a: a.reshape(-1, a.shape[-1])
    k_o, v_o, q, da = proj_call(
        True, sc, normed, dy, flat(cos_o), flat(sin_o), qkv_half, out_half, got_qkv, got_out
    )
    k_p, v_p = proj_call(
        False, sc, before, dy, flat(cos_p), flat(sin_p), qkv_half, out_half, got_qkv, got_out
    )
    per_seq = lambda a: a.reshape(2, -1, HALF)
    att, dq, dko, dkp, dvo, dvp = attend_call(
        sc,
        per_seq(q),
        per_seq(da),
        per_seq(k_o),
        per_seq(k_p),
        per_seq(v_o),
        per_seq(v_p),
        first[..., None],
        cos_o,
        sin_o,
        cos_p,
        sin_p,
    )
    attn_o, dn_a, dn_p, g_qkv, g_out = back_call(
        sc,
        normed,
        before,
        dy,
        flat(att),
        flat(dq),
        flat(dko),
        flat(dvo),
        flat(dkp),
        flat(dvp),
        qkv_half,
        out_half,
        got_qkv,
        got_out,
    )
    qkv_parts = jnp.transpose(g_qkv.reshape(SHARDS, 2, 2, 64, 3 * HALF), (1, 0, 2, 3, 4))
    out_parts = jnp.transpose(g_out.reshape(SHARDS, 2, 2, 32, D), (1, 0, 2, 3, 4))
    qkv_done = finish(reduce(qkv_parts, True), True)
    out_done = finish(reduce(out_parts, False), False)

    outs = (mlp_sum[0].astype(full) + mlp_sum[1].astype(full) + attn_o.astype(full)).reshape(
        2, rows, D
    )
    inputs = tokens.astype(full)
    mixed = (inputs + outs[0] + swap(outs[1].astype(low), 1).astype(full) + bfc).astype(low)

    dn = (dn_sum[0].astype(full) + dn_sum[1].astype(full) + dn_a.astype(full)).reshape(2, rows, D)
    dn_p = dn_p.reshape(2, 2, rows, D)
    prior = add(dn_p[0], swap(dn_p[1], 1))
    mine = dn[0] + swap(dn[1].astype(low), 1).astype(full)
    joined = add(prior[1], downward(prior[0]))
    total = mine + downward(joined).astype(full)

    n_mine = (inputs - mean[0]) * rstd[0]
    n_prior = (early[0].astype(full) - mean_p[0]) * rstd_p[0]
    prior_full = prior.astype(full)
    d_gain = jnp.sum(mine * n_mine, axis=0) + jnp.sum(prior_full * n_prior, axis=(0, 1))
    d_shift = jnp.sum(mine, axis=0) + jnp.sum(prior_full, axis=(0, 1))
    g = total * gain
    d_in = rstd[0] * (
        g
        - jnp.mean(g, axis=-1, keepdims=True)
        - n_mine * jnp.mean(g * n_mine, axis=-1, keepdims=True)
    )
    dy_full = cotangent.astype(full)
    grad_tokens = (dy_full + d_in).astype(low)

    d_bfc = jnp.sum(dy_full, axis=0)
    d_bin = jnp.stack(bin_parts, axis=1)
    zero = jnp.zeros_like(d_bin)
    d_bin = jnp.stack(
        [jnp.where(c == 0, d_bin, zero), jnp.where(c == 0, zero, d_bin)], axis=1
    ).reshape(SHARDS, -1)
    v = jnp.concatenate(
        [d_gain.reshape(SHARDS, -1), d_shift.reshape(SHARDS, -1), d_bfc.reshape(SHARDS, -1), d_bin],
        axis=1,
    )
    bit = 1
    while bit < reps:
        v = v + swap(v, bit)
        bit *= 2
    for s in (1, 2):
        v = v + lax.ppermute(v, "shard", [(i, i ^ s) for i in range(SHARDS)])
    v = pick(v, z, 0)

    fc_rows, in_rows = [], []
    for k in range(CHUNKS):
        a = grads_mlp[k].reshape(2, 2, 2, 128, WIDE)
        in_rows.append(a[:, 0].reshape(2, quart, SHARDS, PART))
        fc_rows.append(a[:, 1].reshape(2, PART, D))
    grad_in = jnp.transpose(jnp.stack(in_rows), (2, 3, 1, 0, 4)).reshape(quart, FF).astype(full)
    grad_fc = jnp.transpose(jnp.stack(fc_rows), (1, 0, 2, 3)).reshape(D, D).astype(full)
    grad_qkv = (
        jnp.transpose(qkv_done.reshape(2, quart, 3 * PAIRS, 128), (1, 2, 0, 3))
        .reshape(quart, 3 * D)
        .astype(full)
    )
    grad_out = out_done.reshape(quart, D).astype(full)
    return (
        mixed,
        grad_tokens,
        v[:quart],
        v[quart : 2 * quart],
        grad_qkv,
        grad_out,
        grad_in,
        v[3 * quart :],
        grad_fc,
        v[2 * quart : 3 * quart],
    )


def solution(mesh):
    return jax.shard_map(
        functools.partial(on_device, mesh.shape["rep"]),
        mesh=mesh,
        in_specs=(
            P(("rep", "shard"), None),
            P(("rep", "shard")),
            P("shard"),
            P("shard"),
            P("shard", None),
            P("shard", None),
            P("shard", None),
            P("shard"),
            P("shard", None),
            P("shard"),
            P(("rep", "shard"), None),
        ),
        out_specs=(
            P(("rep", "shard"), None),
            P(("rep", "shard"), None),
            P("shard"),
            P("shard"),
            P("shard", None),
            P("shard", None),
            P("shard", None),
            P("shard"),
            P("shard", None),
            P("shard"),
        ),
        check_vma=False,
    )
```
